128 devices in a mesh: dp: 16 (over x_lo, y, core), shard: 8 (over x_hi, z).
Axes of the slice: x: 4 (x_hi: 2, x_lo: 2; x = x_hi * 2 + x_lo), y: 4, z: 4, core: 2. Of those that a mesh axis runs over, the one named last changes fastest.
Arguments:
- grad_parts: bfloat16 [16, 16, 1024, 1024], P('dp', None, 'shard'), may hold values from -6 to 6
- first_moment: float32 [16384, 1024], P(('dp', 'shard')), may hold values from -6 to 6
- second_moment: float32 [16384, 1024], P(('dp', 'shard')), may hold values from 0.1 to 16
- master: float32 [16384, 1024], P(('dp', 'shard')), may hold values from -6 to 6
- old_map: int32 [16384], replicated, may hold values from 0 to 16383, as said below
- new_map: int32 [16384], replicated, may hold values from 0 to 16383, as said below
Outputs:
- new_first: float32 [16384, 1024], P(('dp', 'shard'))
- new_second: float32 [16384, 1024], P(('dp', 'shard'))
- new_master: float32 [16384, 1024], P(('dp', 'shard'))
- weights_half: bfloat16 [16384, 1024], P('dp')
The draws below stay inside these ranges and needn't reach their ends.
Inputs may be any that keep to these rules, and one draw needn't show every extreme that they name: old_map is a permutation of the 16384 block numbers. Row r of either layout belongs to device r // 128. Of the blocks that one device holds in the old layout, exactly one belongs to each device in the new layout. new_map is a permutation of the 16384 block numbers, with the property stated for old_map.
All inputs are finite; a program needn't handle non-finite values.
Results may differ from the reference program's by a relative error of at most 0.0085.
Values may be sent and summed in bfloat16 or wider, within the bound.
A program may use at most 64 MiB of HBM per device.

```python
import math
import jax
import jax.numpy as jnp
from jax import lax

BPD = 128
BLK = 1024
BLOCKS = 16384
N_DP = 16
N_SHARD = 8


def shuffle_rows(subkey, table):
    side = table.shape[0]
    orders = jax.vmap(lambda inner: jax.random.permutation(inner, table.shape[1]))(jax.random.split(subkey, side))
    return jnp.take_along_axis(table, orders, axis=1)


def relayout_maps(key):
    key_list = jax.random.split(jax.random.fold_in(key, 7), 5)
    side = BPD
    row_perm = jax.random.permutation(key_list[0], side)
    col_perm = jax.random.permutation(key_list[1], side)
    dests = (row_perm[:, None] + col_perm[None, :]) % side
    dests = shuffle_rows(key_list[2], dests)
    flat_dest = dests.reshape(-1)
    labels = jax.random.permutation(key_list[3], BPD * BPD)
    grouped = jnp.argsort(flat_dest, stable=True).reshape(BPD, BPD)
    grouped = shuffle_rows(key_list[4], grouped)
    return (labels.astype(jnp.int32), labels[grouped.reshape(-1)].astype(jnp.int32))


def draw_old_map(key, part):
    return relayout_maps(key)[0]


def draw_new_map(key, part):
    return relayout_maps(key)[1]


def with_spikes(entries, own_key, source, target, shards_of, factor):
    owner, partner = [(jnp.arange(entries.shape[axis_at]) // (entries.shape[axis_at] // shards_of)).reshape([-1 if axis == axis_at else 1 for axis in range(entries.ndim)]) for axis_at in (source, target)]
    chosen = jax.random.permutation(own_key, shards_of)[partner]
    strong = (owner == chosen) | (owner == (partner + shards_of // 2) % shards_of)
    return jnp.where(strong, factor * entries, entries)


def levels(stream_key, extent, shards, least, top_value):
    factor_of, own = 1.0, jax.random.fold_in(stream_key, 6)
    for dim, parts in shards:
        draws = jnp.exp(jax.random.uniform(jax.random.fold_in(own, dim), (parts,), jnp.float32, least / len(shards), top_value / len(shards)))
        factor_of = factor_of * jnp.repeat(draws, extent[dim] // parts).reshape([-1 if axis == dim else 1 for axis in range(len(extent))])
    return factor_of


def centred(key, extent, deviation, most, cuts=(), kind=jnp.bfloat16):
    values = jax.random.normal(key, extent, jnp.float32) * deviation
    if len(cuts) > 0:
        values = levels(key, extent, cuts, -0.22, 0.18) * values
    return jnp.clip(values, min=-most, max=most).astype(kind)


def heavy_noise(own_key, dims, scale, limit, cuts, heavy, kind=jnp.bfloat16):
    result = scale * jax.random.normal(own_key, dims, jnp.float32)
    if cuts:
        result = result * levels(own_key, dims, cuts, -0.22, 0.18)
    return jnp.clip(with_spikes(result, jax.random.fold_in(own_key, 3), *heavy), -limit, limit).astype(kind)


def setup_inputs(seed: int = 0) -> dict:
    splits = jax.random.split(jax.random.key(seed), 7)
    return {
        "grad_parts": heavy_noise(splits[0], (N_DP, N_DP, N_SHARD * BPD, BLK), 1.0, 6.0, ((0, 16), (2, 8)), (0, 1, 16, 2.0)),
        "first_moment": centred(splits[1], (BLOCKS, BLK), 1.0, 6.0, ((0, 128),), jnp.float32),
        "second_moment": jnp.clip(jnp.exp(math.log(16.0) - 5.075174 * jax.random.uniform(splits[2], (BLOCKS, BLK), jnp.float32) ** levels(splits[2], (BLOCKS, BLK), ((0, 128),), -0.2, 0.2)), 0.1, 16.0),
        "master": centred(splits[3], (BLOCKS, BLK), 1.0, 6.0, ((0, 128),), jnp.float32),
        "old_map": draw_old_map(jax.random.fold_in(splits[6], 71), 0),
        "new_map": draw_new_map(jax.random.fold_in(splits[6], 71), 0),
    }


beta_one = 0.9
beta_two = 0.95
learning_rate = 0.05
decay_rate = 0.1
epsilon = 1e-08
step_count = 4

def adamw(moment_one, moment_two, weights, gradient):
    new_one = beta_one * moment_one + (1.0 - beta_one) * gradient
    new_two = beta_two * moment_two + (1.0 - beta_two) * gradient * gradient
    unbiased_one = new_one / (1.0 - beta_one ** step_count)
    unbiased_two = new_two / (1.0 - beta_two ** step_count)
    updated = weights - learning_rate * (unbiased_one / (jnp.sqrt(unbiased_two) + epsilon) + decay_rate * weights)
    return (new_one, new_two, updated)

def reference(grad_parts, first_moment, second_moment, master, old_map, new_map):

    def add_part(index, running):
        piece = lax.dynamic_index_in_dim(grad_parts, index, 0, keepdims=False)
        return running + piece.astype(jnp.float32)
    summed = lax.fori_loop(0, grad_parts.shape[0], add_part, jnp.zeros(grad_parts.shape[1:], jnp.float32))
    summed = summed.reshape(-1, summed.shape[-1])
    row_count = old_map.shape[0]
    old_place = jnp.zeros((row_count,), jnp.int32).at[old_map].set(jnp.arange(row_count, dtype=jnp.int32))
    source = old_place[new_map].astype(jnp.int32)
    new_one, new_two, updated = adamw(first_moment[source], second_moment[source], master[source], summed)
    return (new_one, new_two, updated, updated.astype(jnp.bfloat16))
```

```python
import functools

import jax
import jax.numpy as jnp
from jax import lax
from jax.experimental import pallas as pl
from jax.experimental.pallas import tpu as pltpu
from jax.sharding import PartitionSpec as P

beta_one = 0.9
beta_two = 0.95
learning_rate = 0.05
decay_rate = 0.1
epsilon = 1e-08
step_count = 4

MESH = pl.DeviceIdType.MESH
BPD = 128
BLK = 1024
f32 = jnp.float32
bf16 = jnp.bfloat16

CHUNKS = ((0, 32, "y", "x"), (32, 32, "x", "z"), (64, 32, "y", "x"), (96, 32, "x", "z"))


def adamw(moment_one, moment_two, weights, gradient):
    new_one = beta_one * moment_one + (1.0 - beta_one) * gradient
    new_two = beta_two * moment_two + (1.0 - beta_two) * gradient * gradient
    unbiased_one = new_one / (1.0 - beta_one**step_count)
    unbiased_two = new_two / (1.0 - beta_two**step_count)
    updated = weights - learning_rate * (
        unbiased_one / (jnp.sqrt(unbiased_two) + epsilon) + decay_rate * weights
    )
    return (new_one, new_two, updated)


def owners(wanted_row, table_ref, turned_ref):
    wanted = jnp.broadcast_to(wanted_row, (BPD, BPD)).T
    turned_ref[...] = table_ref[...].T

    def step(k, found):
        return jnp.where(wanted == turned_ref[pl.ds(k, 1), :], 1.0, found)

    return lax.fori_loop(0, BPD, step, jnp.zeros((BPD, BPD), f32), unroll=8)


def swap_matrix():
    row = lax.broadcasted_iota(jnp.int32, (BPD, BPD), 0)
    col = lax.broadcasted_iota(jnp.int32, (BPD, BPD), 1)
    turned = (row & 64) | ((row & 7) << 3) | ((row >> 3) & 7)
    return jnp.where(turned == col, 1.0, 0.0).astype(bf16)


def kernel(
    grad, first, second, master, old_map, new_map,
    out_one, out_two, out_master, out_half,
    states, old_ref, new_ref, turned, own, other, pair, from_y, from_x, part, kept,
    send_a, recv_a, send_b, recv_b,
    load_sem, core_s, core_r, sum_s, sum_r, a_s, a_r, b_s, b_r, gat_s, gat_r, fwd_s, fwd_r,
):
    dp = lax.axis_index("dp")
    sh = lax.axis_index("shard")
    xl, yc = dp // 8, dp % 8
    y, c = yc // 2, yc % 2
    xh, z = sh // 4, sh % 4
    me = dp * 8 + sh

    def at_y(k):
        return (xl * 8 + lax.rem(y + k, 4) * 2 + c, sh)

    def at_z(k):
        return (dp, xh * 4 + lax.rem(z + k, 4))

    x_near = ((1 - xl) * 8 + yc, sh)
    x_far = (dp, (1 - xh) * 4 + z)
    core_mate = (xl * 8 + y * 2 + (1 - c), sh)
    a_peers = [(xl * 8 + lax.rem(yc + k, 8), sh) for k in range(1, 8)]
    place = xl * 8 + sh
    b_places = [lax.rem(place + k, 16) for k in range(1, 16)]
    b_peers = [((p // 8) * 8 + yc, p % 8) for p in b_places]

    barrier = pltpu.get_barrier_semaphore()
    for peer in a_peers + b_peers:
        pl.semaphore_signal(barrier, inc=1, device_id=peer, device_id_type=MESH)

    loads = [
        pltpu.make_async_copy(new_map, new_ref, load_sem.at[0]),
        pltpu.make_async_copy(old_map, old_ref, load_sem.at[1]),
        pltpu.make_async_copy(first, states.at[0], load_sem.at[2]),
        pltpu.make_async_copy(second, states.at[1], load_sem.at[3]),
        pltpu.make_async_copy(master, states.at[2], load_sem.at[4]),
        pltpu.make_async_copy(grad.at[:, c], own, load_sem.at[5]),
    ]
    for load in loads:
        load.start()
    loads[0].wait()
    loads[1].wait()
    route = owners(old_ref[pl.ds(me, 1), :], new_ref, turned).T.astype(bf16)

    pl.semaphore_wait(barrier, 22)

    def remote(src, dst, s_sem, r_sem, peer):
        copy = pltpu.make_async_remote_copy(
            src_ref=src, dst_ref=dst, send_sem=s_sem, recv_sem=r_sem,
            device_id=peer, device_id_type=MESH,
        )
        copy.start()
        return copy

    sent = []

    core = []
    for i, (r0, n, _, _) in enumerate(CHUNKS):
        rows = pl.ds(r0, n)
        core.append(
            remote(grad.at[:, 1 - c, rows], other.at[:, rows], core_s.at[i], core_r.at[i], core_mate)
        )
    sent += core

    for j in range(3):
        loads[2 + j].wait()
        moved = jnp.dot(route, states[j].astype(bf16), preferred_element_type=f32)
        send_a[:, :, :, j * BLK : (j + 1) * BLK] = moved.reshape(2, 8, 8, BLK).astype(bf16)
    stage_a = []
    for k in range(1, 8):
        to = lax.rem(yc + k, 8)
        stage_a.append(
            remote(send_a.at[:, to], recv_a.at[:, yc], a_s.at[k - 1], a_r.at[k - 1], a_peers[k - 1])
        )
    sent += stage_a
    keep_a = pltpu.make_async_copy(send_a.at[:, yc], recv_a.at[:, yc], load_sem.at[0])
    keep_a.start()

    loads[5].wait()
    steps_one = []
    for i, (r0, n, order, _) in enumerate(CHUNKS):
        rows = pl.ds(r0, n)
        core[i].wait_recv()

        def add_pair(q, carry, rows=rows):
            pair[q, rows, :] = own[q, rows, :] + other[q, rows, :]
            return carry

        lax.fori_loop(0, 8, add_pair, 0)
        if order == "x":
            copies = [
                remote(
                    pair.at[pl.ds((1 - xl) * 4, 4), rows], from_x.at[:, rows],
                    sum_s.at[i, 0], sum_r.at[i, 0], x_near,
                )
            ]
        else:
            copies = []
            for k in range(1, 4):
                to = lax.rem(y + k, 4)
                for side in range(2):
                    copies.append(
                        remote(
                            pair.at[side * 4 + to, rows], from_y.at[k - 1, side, rows],
                            sum_s.at[i, (k - 1) * 2 + side], sum_r.at[i, (k - 1) * 2 + side], at_y(k),
                        )
                    )
        steps_one.append(copies)
        sent += copies

    swap = swap_matrix()
    for copy in stage_a:
        copy.wait_recv()
    keep_a.wait()
    for j in range(3):
        cols = slice(j * BLK, (j + 1) * BLK)
        came = recv_a[:, :, :, cols].astype(f32).reshape(BPD, BLK).astype(bf16)
        moved = jnp.dot(swap, came, preferred_element_type=f32)
        send_b[:, :, cols] = moved.reshape(16, 8, BLK).astype(bf16)
    stage_b = []
    for k in range(1, 16):
        stage_b.append(
            remote(send_b.at[b_places[k - 1]], recv_b.at[place], b_s.at[k - 1], b_r.at[k - 1], b_peers[k - 1])
        )
    sent += stage_b
    keep_b = pltpu.make_async_copy(send_b.at[place], recv_b.at[place], load_sem.at[1])
    keep_b.start()

    steps_two = []
    for i, (r0, n, order, _) in enumerate(CHUNKS):
        rows = pl.ds(r0, n)
        for copy in steps_one[i]:
            copy.wait_recv()
        copies = []
        if order == "x":
            for k in range(1, 4):
                to = lax.rem(y + k, 4)
                part[k - 1, rows, :] = pair[xl * 4 + to, rows, :] + from_x[to, rows, :]
                copies.append(
                    remote(
                        part.at[k - 1, rows], from_y.at[k - 1, 0, rows],
                        sum_s.at[i, k], sum_r.at[i, k], at_y(k),
                    )
                )
            kept[rows, :] = pair[xl * 4 + y, rows, :].astype(f32) + from_x[y, rows, :].astype(f32)
        else:
            def total(side, rows=rows):
                value = pair[side * 4 + y, rows, :].astype(f32)
                for k in range(3):
                    value = value + from_y[k, side, rows, :].astype(f32)
                return value

            part[0, rows, :] = total(1 - xl).astype(bf16)
            copies.append(
                remote(part.at[0, rows], from_x.at[0, rows], sum_s.at[i, 6], sum_r.at[i, 6], x_near)
            )
            kept[rows, :] = total(xl)
        steps_two.append(copies)
        sent += copies

    pick = owners(new_ref[pl.ds(me, 1), :], old_ref, turned).astype(bf16)
    pick = jnp.dot(pick, swap, preferred_element_type=f32).astype(bf16)
    for copy in stage_b:
        copy.wait_recv()
    keep_b.wait()
    for j in range(3):
        cols = slice(j * BLK, (j + 1) * BLK)
        came = recv_b[:, :, cols].astype(f32).reshape(BPD, BLK).astype(bf16)
        states[j] = jnp.dot(pick, came, preferred_element_type=f32)

    gathers = []
    for i, (r0, n, order, _) in enumerate(CHUNKS):
        rows = pl.ds(r0, n)
        for copy in steps_two[i]:
            copy.wait_recv()
        summed = kept[rows, :]
        if order == "x":
            for k in range(3):
                summed = summed + from_y[k, 0, rows, :].astype(f32)
        else:
            summed = summed + from_x[0, rows, :].astype(f32)
        new_one, new_two, updated = adamw(
            states[0, rows, :], states[1, rows, :], states[2, rows, :], summed
        )
        out_half[sh, rows, :] = updated.astype(bf16)
        block = out_half.at[sh, rows]
        copies = [remote(block, block, gat_s.at[i, 0], gat_r.at[i, 0], x_far)]
        for k in range(1, 4):
            copies.append(remote(block, block, gat_s.at[i, k], gat_r.at[i, k], at_z(k)))
        gathers.append(copies)
        sent += copies
        out_one[rows, :] = new_one
        out_two[rows, :] = new_two
        out_master[rows, :] = updated

    forwards = []
    for i, (r0, n, _, order) in enumerate(CHUNKS):
        rows = pl.ds(r0, n)
        copies = []
        if order == "x":
            gathers[i][0].wait_recv()
            block = out_half.at[(1 - xh) * 4 + z, rows]
            for k in range(1, 4):
                copies.append(remote(block, block, fwd_s.at[i, k - 1], fwd_r.at[i, k - 1], at_z(k)))
        for k in range(1, 4):
            gathers[i][k].wait_recv()
            if order == "z":
                block = out_half.at[xh * 4 + lax.rem(z + 4 - k, 4), rows]
                copies.append(remote(block, block, fwd_s.at[i, k - 1], fwd_r.at[i, k - 1], x_far))
        if order == "z":
            gathers[i][0].wait_recv()
        forwards.append(copies)
        sent += copies
    for copies in forwards:
        for copy in copies:
            copy.wait_recv()
    for copy in sent:
        copy.wait_send()


def fused(grad, first, second, master, old_map, new_map):
    chunks = len(CHUNKS)
    rows = jax.ShapeDtypeStruct((BPD, BLK), f32)
    anywhere = pl.BlockSpec(memory_space=pl.ANY)
    near = pl.BlockSpec(memory_space=pltpu.VMEM)
    sem = pltpu.SemaphoreType.DMA
    return pl.pallas_call(
        kernel,
        out_shape=(rows, rows, rows, jax.ShapeDtypeStruct((8, BPD, BLK), bf16)),
        in_specs=[anywhere] * 6,
        out_specs=(near,) * 4,
        scratch_shapes=[
            pltpu.VMEM((3, BPD, BLK), f32),
            pltpu.VMEM((BPD, BPD), jnp.int32),
            pltpu.VMEM((BPD, BPD), jnp.int32),
            pltpu.VMEM((BPD, BPD), jnp.int32),
            pltpu.VMEM((8, BPD, BLK), bf16),
            pltpu.VMEM((8, BPD, BLK), bf16),
            pltpu.VMEM((8, BPD, BLK), bf16),
            pltpu.VMEM((3, 2, BPD, BLK), bf16),
            pltpu.VMEM((4, BPD, BLK), bf16),
            pltpu.VMEM((3, BPD, BLK), bf16),
            pltpu.VMEM((BPD, BLK), f32),
            pltpu.VMEM((2, 8, 8, 3 * BLK), bf16),
            pltpu.VMEM((2, 8, 8, 3 * BLK), bf16),
            pltpu.VMEM((16, 8, 3 * BLK), bf16),
            pltpu.VMEM((16, 8, 3 * BLK), bf16),
            sem((6,)),
            sem((chunks,)), sem((chunks,)),
            sem((chunks, 7)), sem((chunks, 7)),
            sem((7,)), sem((7,)),
            sem((15,)), sem((15,)),
            sem((chunks, 4)), sem((chunks, 4)),
            sem((chunks, 3)), sem((chunks, 3)),
        ],
        compiler_params=pltpu.CompilerParams(
            collective_id=0, has_side_effects=True, vmem_limit_bytes=48 * 1024 * 1024
        ),
        name="adamw_relayout",
    )(grad, first, second, master, old_map, new_map)


def local(grad_parts, first_moment, second_moment, master, old_map, new_map):
    new_one, new_two, updated, half = fused(
        grad_parts.reshape(8, 2, BPD, BLK),
        first_moment,
        second_moment,
        master,
        old_map.reshape(BPD, BPD),
        new_map.reshape(BPD, BPD),
    )
    return (new_one, new_two, updated, half.reshape(8 * BPD, BLK))


def solution(mesh):
    placed = (
        P("dp", None, "shard", None),
        P(("dp", "shard"), None),
        P(("dp", "shard"), None),
        P(("dp", "shard"), None),
        P(),
        P(),
    )
    return jax.shard_map(
        local,
        mesh=mesh,
        in_specs=placed,
        out_specs=(
            P(("dp", "shard"), None),
            P(("dp", "shard"), None),
            P(("dp", "shard"), None),
            P("dp", None),
        ),
        check_vma=False,
    )
```

```python
import functools

import jax
import jax.numpy as jnp
from jax import lax
from jax.experimental import pallas as pl
from jax.experimental.pallas import tpu as pltpu
from jax.sharding import PartitionSpec as P

beta_one = 0.9
beta_two = 0.95
learning_rate = 0.05
decay_rate = 0.1
epsilon = 1e-08
step_count = 4

MESH = pl.DeviceIdType.MESH
BPD = 128
BLK = 1024
f32 = jnp.float32
bf16 = jnp.bfloat16

CHUNKS = ((0, 16, 'x', 'z'), (16, 16, 'x', 'X'), (32, 16, 'x', 'z'), (48, 16, 'y', 'x'), (64, 32, 'Y', 'z'), (96, 32, 'Y', 'X'))
ORDER = (
    "A0", "P1", "A1", "P2", "P4", "P5", "T0", "R4", "R5", "T1", "pick", "Q4",
    "Q5", "P0", "P3", "S0", "S1", "U4", "Q2", "U5", "Q3", "U2", "Q1", "G4",
    "Q0", "G5", "U1", "U3", "U0", "G2", "G1", "G3", "G0", "H5", "H1",
)
PIECES = ((0, 0, 1024, 0, 0), (1, 0, 512, 0, 1024), (1, 512, 512, 1, 0), (2, 0, 1024, 1, 512))


def adamw(moment_one, moment_two, weights, gradient):
    new_one = beta_one * moment_one + (1.0 - beta_one) * gradient
    new_two = beta_two * moment_two + (1.0 - beta_two) * gradient * gradient
    unbiased_one = new_one / (1.0 - beta_one**step_count)
    unbiased_two = new_two / (1.0 - beta_two**step_count)
    updated = weights - learning_rate * (
        unbiased_one / (jnp.sqrt(unbiased_two) + epsilon) + decay_rate * weights
    )
    return (new_one, new_two, updated)


def owners(wanted_row, table_ref, turned_ref):
    wanted = jnp.broadcast_to(wanted_row, (BPD, BPD)).T
    turned_ref[...] = table_ref[...].T

    def step(k, found):
        return jnp.where(wanted == turned_ref[pl.ds(k, 1), :], 1.0, found)

    return lax.fori_loop(0, BPD, step, jnp.zeros((BPD, BPD), f32), unroll=8)


def swap_matrix():
    row = lax.broadcasted_iota(jnp.int32, (BPD, BPD), 0)
    col = lax.broadcasted_iota(jnp.int32, (BPD, BPD), 1)
    turned = (row & 64) | ((row & 7) << 3) | ((row >> 3) & 7)
    return jnp.where(turned == col, 1.0, 0.0).astype(bf16)


def kernel(
    grad, first, second, master, old_map, new_map,
    out_one, out_two, out_master, out_half,
    states, old_ref, new_ref, turned, own, other, pair, from_y, from_x, part, kept,
    send_a, recv_a, send_b, recv_b,
    load_sem, core_s, core_r, sum_s, sum_r, a_s, a_r, b_s, b_r, gat_s, gat_r, fwd_s, fwd_r,
):
    dp = lax.axis_index("dp")
    sh = lax.axis_index("shard")
    xl, yc = dp // 8, dp % 8
    y, c = yc // 2, yc % 2
    xh, z = sh // 4, sh % 4
    me = dp * 8 + sh

    def at_y(k):
        return (xl * 8 + lax.rem(y + k, 4) * 2 + c, sh)

    def at_z(k):
        return (dp, xh * 4 + lax.rem(z + k, 4))

    x_near = ((1 - xl) * 8 + yc, sh)
    x_far = (dp, (1 - xh) * 4 + z)
    core_mate = (xl * 8 + y * 2 + (1 - c), sh)
    a_places = [lax.rem(yc + k, 8) for k in range(1, 8)]
    a_peers = [(xl * 8 + p, sh) for p in a_places]
    place = xl * 8 + sh
    b_places = [lax.rem(place + k, 16) for k in range(1, 16)]
    b_peers = [((p // 8) * 8 + yc, p % 8) for p in b_places]

    barrier = pltpu.get_barrier_semaphore()
    for peer in a_peers + b_peers:
        pl.semaphore_signal(barrier, inc=1, device_id=peer, device_id_type=MESH)

    loads = [
        pltpu.make_async_copy(new_map, new_ref, load_sem.at[0]),
        pltpu.make_async_copy(old_map, old_ref, load_sem.at[1]),
        pltpu.make_async_copy(first, states.at[0], load_sem.at[2]),
        pltpu.make_async_copy(second, states.at[1], load_sem.at[3]),
        pltpu.make_async_copy(master, states.at[2], load_sem.at[4]),
        pltpu.make_async_copy(grad.at[:, c], own, load_sem.at[5]),
    ]
    for load in loads:
        load.start()
    loads[0].wait()
    loads[1].wait()
    swap = swap_matrix()
    route = owners(old_ref[pl.ds(me, 1), :], new_ref, turned).T.astype(bf16)
    routes = (route, jnp.dot(swap, route, preferred_element_type=f32).astype(bf16))

    pl.semaphore_wait(barrier, 22)

    def remote(src, dst, s_sem, r_sem, peer):
        copy = pltpu.make_async_remote_copy(
            src_ref=src, dst_ref=dst, send_sem=s_sem, recv_sem=r_sem,
            device_id=peer, device_id_type=MESH,
        )
        copy.start()
        return copy

    sent = []

    core = []
    for i, (r0, n, _, _) in enumerate(CHUNKS):
        rows = pl.ds(r0, n)
        core.append(
            remote(grad.at[:, 1 - c, rows], other.at[:, rows], core_s.at[i], core_r.at[i], core_mate)
        )
    sent += core

    def over_a(lane):
        for k in range(7):
            (
                remote(
                    send_a.at[lane, :, a_places[k]], recv_a.at[lane, :, yc],
                    a_s.at[lane], a_r.at[lane], a_peers[k],
                )
            )
        whole = pltpu.make_async_remote_copy(
            src_ref=send_a.at[lane, :, pl.ds(0, 7)], dst_ref=recv_a.at[lane, :, pl.ds(0, 7)],
            send_sem=a_s.at[lane], recv_sem=a_r.at[lane], device_id=a_peers[0], device_id_type=MESH,
        )
        keep = pltpu.make_async_copy(send_a.at[lane, :, yc], recv_a.at[lane, :, yc], load_sem.at[lane])
        keep.start()
        return [whole], keep

    def over_b(lane):
        for k in range(15):
            (
                remote(
                    send_b.at[lane, b_places[k]], recv_b.at[lane, place],
                    b_s.at[lane], b_r.at[lane], b_peers[k],
                )
            )
        whole = pltpu.make_async_remote_copy(
            src_ref=send_b.at[lane, pl.ds(0, 15)], dst_ref=recv_b.at[lane, pl.ds(0, 15)],
            send_sem=b_s.at[lane], recv_sem=b_r.at[lane], device_id=b_peers[0], device_id_type=MESH,
        )
        keep = pltpu.make_async_copy(send_b.at[lane, place], recv_b.at[lane, place], load_sem.at[6 + lane])
        keep.start()
        return [whole], keep

    def arrived(stage):
        for copy in stage[0]:
            copy.wait_recv()
        stage[1].wait()

    def set_out(lane):
        for j, c0, w, of, l0 in PIECES:
            if of == lane:
                if j in pending:
                    pending.pop(j).wait()
                moved = jnp.dot(
                    routes[lane], states[j, :, c0 : c0 + w].astype(bf16), preferred_element_type=f32
                )
                if lane == 0:
                    send_a[0, :, :, :, l0 : l0 + w] = moved.reshape(2, 8, 8, w).astype(bf16)
                else:
                    send_b[1, :, :, l0 : l0 + w] = moved.reshape(16, 8, w).astype(bf16)
        stage_one[lane] = over_a(0) if lane == 0 else over_b(1)
        sent.extend(stage_one[lane][0])

    steps_one, steps_two, gathers, forwards = {}, {}, {}, {}

    def pairs(i):
        r0, n, order, _ = CHUNKS[i]
        rows = pl.ds(r0, n)
        core[i].wait_recv()
        if 3 in pending:
            pending.pop(3).wait()

        def add_pair(q, carry):
            pair[q // 4, q % 4, rows, :] = own[q, rows, :] + other[q, rows, :]
            return carry

        lax.fori_loop(0, 8, add_pair, 0)
        if order == "x":
            copies = [
                remote(pair.at[1 - xl, :, rows], from_x.at[:, rows], sum_s.at[i, 0], sum_r.at[i, 0], x_near)
            ]
        elif order == "d":
            copies = [
                remote(pair.at[1 - xl, y, rows], from_x.at[0, rows], sum_s.at[i, 6], sum_r.at[i, 6], x_near)
            ]
            for k in range(1, 4):
                for side, there in ((0, xl), (1, 1 - xl)):
                    to = lax.rem(y + k, 4)
                    copies.append(
                        remote(
                            pair.at[there, to, rows], from_y.at[k - 1, side, rows],
                            sum_s.at[i, side * 3 + k - 1], sum_r.at[i, side * 3 + k - 1],
                            (there * 8 + to * 2 + c, sh),
                        )
                    )
        elif order == "y":
            copies = []
            for k in range(1, 4):
                copies.append(
                    remote(
                        pair.at[:, lax.rem(y + k, 4), rows], from_y.at[k - 1, :, rows],
                        sum_s.at[i, k - 1], sum_r.at[i, k - 1], at_y(k),
                    )
                )
        else:
            low, high = pl.ds(r0, n // 2), pl.ds(r0 + n // 2, n // 2)
            copies = []
            for k, to, half, slot, peer in (
                (0, 2, low, 1, 1), (1, 2, high, 1, 3), (2, 1, high, 0, 1), (3, 3, low, 2, 3)
            ):
                copies.append(
                    remote(
                        pair.at[:, lax.rem(y + to, 4), half], from_y.at[slot, :, half],
                        sum_s.at[i, k], sum_r.at[i, k], at_y(peer),
                    )
                )
        steps_one[i] = copies
        sent.extend(copies)

    def relay(i):
        r0, n, _, _ = CHUNKS[i]
        for k, to, half in ((0, 1, pl.ds(r0, n // 2)), (1, 3, pl.ds(r0 + n // 2, n // 2))):
            steps_one[i][k].wait_recv()
            place_y = lax.rem(y + to, 4)
            for side in range(2):
                pair[side, place_y, half, :] = pair[side, place_y, half, :] + from_y[1, side, half, :]
            copy = remote(
                pair.at[:, place_y, half], from_y.at[to - 1, :, half],
                sum_s.at[i, 4 + k], sum_r.at[i, 4 + k], at_y(to),
            )
            steps_one[i].append(copy)
            sent.append(copy)
        del steps_one[i][:2]

    def second_axis(i):
        r0, n, order, _ = CHUNKS[i]
        rows = pl.ds(r0, n)
        for copy in steps_one[i]:
            copy.wait_recv()
        copies = []
        if order == "d":
            value = pair[xl, y, rows, :].astype(f32) + from_x[0, rows, :].astype(f32)
            for k in range(3):
                for side in range(2):
                    value = value + from_y[k, side, rows, :].astype(f32)
            kept[rows, :] = value
        elif order == "x":
            for k in range(1, 4):
                to = lax.rem(y + k, 4)
                part[k - 1, rows, :] = pair[xl, to, rows, :] + from_x[to, rows, :]
                copies.append(
                    remote(
                        part.at[k - 1, rows], from_y.at[k - 1, 0, rows],
                        sum_s.at[i, k], sum_r.at[i, k], at_y(k),
                    )
                )
            kept[rows, :] = pair[xl, y, rows, :].astype(f32) + from_x[y, rows, :].astype(f32)
        else:
            def total(side):
                value = pair[side, y, rows, :].astype(f32)
                for k in (0, 1, 2) if order == "y" else (0, 2):
                    value = value + from_y[k, side, rows, :].astype(f32)
                return value

            part[0, rows, :] = total(1 - xl).astype(bf16)
            copies.append(
                remote(part.at[0, rows], from_x.at[0, rows], sum_s.at[i, 6], sum_r.at[i, 6], x_near)
            )
            kept[rows, :] = total(xl)
        steps_two[i] = copies
        sent.extend(copies)

    def update(i):
        r0, n, order, gather = CHUNKS[i]
        rows = pl.ds(r0, n)
        for copy in steps_two[i]:
            copy.wait_recv()
        summed = kept[rows, :]
        if order == "d":
            pass
        elif order == "x":
            for k in range(3):
                summed = summed + from_y[k, 0, rows, :].astype(f32)
        else:
            summed = summed + from_x[0, rows, :].astype(f32)
        new_one, new_two, updated = adamw(
            states[0, rows, :], states[1, rows, :], states[2, rows, :], summed
        )
        out_half[sh, rows, :] = updated.astype(bf16)
        block = out_half.at[sh, rows]
        copies = [remote(block, block, gat_s.at[i, 0], gat_r.at[i, 0], x_far)]
        for k in (1, 2, 3) if gather in "xzd" else (1, 3):
            copies.append(remote(block, block, gat_s.at[i, k], gat_r.at[i, k], at_z(k)))
        if gather == "d":
            for k in range(1, 4):
                far = (dp, (1 - xh) * 4 + lax.rem(z + k, 4))
                copies.append(remote(block, block, fwd_s.at[i, k - 1], fwd_r.at[i, k - 1], far))
        gathers[i] = copies
        sent.extend(copies)
        out_one[rows, :] = new_one
        out_two[rows, :] = new_two
        out_master[rows, :] = updated

    def forward(i):
        r0, n, _, order = CHUNKS[i]
        rows, low, high = pl.ds(r0, n), pl.ds(r0, n // 2), pl.ds(r0 + n // 2, n // 2)
        first_copies = gathers[i]
        copies = []

        def send(block, k, peer):
            copies.append(remote(block, block, fwd_s.at[i, k], fwd_r.at[i, k], peer))

        def behind(k):
            return lax.rem(z + 4 - k, 4)

        if order == "d":
            forwards[i] = first_copies
            return
        if order == "x":
            first_copies[0].wait_recv()
            for k in range(1, 4):
                send(out_half.at[(1 - xh) * 4 + z, rows], k - 1, at_z(k))
            for k in range(1, 4):
                first_copies[k].wait_recv()
        elif order == "z":
            for k in range(1, 4):
                first_copies[k].wait_recv()
                send(out_half.at[xh * 4 + behind(k), rows], k - 1, x_far)
            first_copies[0].wait_recv()
        elif order == "X":
            first_copies[0].wait_recv()
            for k, peer in ((0, 1), (1, 3)):
                send(out_half.at[(1 - xh) * 4 + z, rows], k, at_z(peer))
            for k, peer, half in ((1, 1, low), (2, 3, high)):
                first_copies[k].wait_recv()
                send(out_half.at[xh * 4 + behind(peer), half], k + 1, at_z(peer))
        else:
            for k, peer, half in ((1, 1, low), (2, 3, high)):
                first_copies[k].wait_recv()
                send(out_half.at[xh * 4 + behind(peer), half], k - 1, at_z(peer))
                send(out_half.at[xh * 4 + behind(peer), rows], k + 1, x_far)
            first_copies[0].wait_recv()
        forwards[i] = copies
        sent.extend(copies)

    def hand_on(i):
        r0, n, _, order = CHUNKS[i]
        rows, low, high = pl.ds(r0, n), pl.ds(r0, n // 2), pl.ds(r0 + n // 2, n // 2)
        copies = []
        if order == "X":
            for k, peer, half in ((0, 1, low), (1, 3, high)):
                forwards[i][k].wait_recv()
                block = out_half.at[(1 - xh) * 4 + lax.rem(z + 4 - peer, 4), half]
                copies.append(remote(block, block, fwd_s.at[i, 4 + k], fwd_r.at[i, 4 + k], at_z(peer)))
        else:
            for k in range(2):
                forwards[i][k].wait_recv()
            block = out_half.at[xh * 4 + lax.rem(z + 2, 4), rows]
            copies.append(remote(block, block, fwd_s.at[i, 4], fwd_r.at[i, 4], x_far))
        forwards[i] = forwards[i][2:] + copies
        sent.extend(copies)

    def turn_around(lanes):
        for lane in lanes:
            arrived(stage_one[lane])
            for _, _, w, of, l0 in PIECES:
                if of == lane:
                    source = recv_a[0, :, :, :, l0 : l0 + w] if lane == 0 else recv_b[1, :, :, l0 : l0 + w]
                    came = source.astype(f32).reshape(BPD, w).astype(bf16)
                    moved = jnp.dot(swap, came, preferred_element_type=f32)
                    if lane == 0:
                        send_b[0, :, :, l0 : l0 + w] = moved.reshape(16, 8, w).astype(bf16)
                    else:
                        send_a[1, :, :, :, l0 : l0 + w] = moved.reshape(2, 8, 8, w).astype(bf16)
            stage_two[lane] = over_b(0) if lane == 0 else over_a(1)
            sent.extend(stage_two[lane][0])

    def pick_states(lanes):
        for lane in lanes:
            arrived(stage_two[lane])
            for j, c0, w, of, l0 in PIECES:
                if of == lane:
                    source = recv_b[0, :, :, l0 : l0 + w] if lane == 0 else recv_a[1, :, :, :, l0 : l0 + w]
                    came = source.astype(f32).reshape(BPD, w).astype(bf16)
                    states[j, :, c0 : c0 + w] = jnp.dot(picks[lane], came, preferred_element_type=f32)

    stage_one, stage_two, picks = {}, {}, []
    pending = dict(enumerate(loads[2:6]))
    for step in ORDER:
        if step == "pick":
            pick = owners(new_ref[pl.ds(me, 1), :], old_ref, turned).astype(bf16)
            picks += [jnp.dot(pick, swap, preferred_element_type=f32).astype(bf16), pick]
        elif step[0] == "A":
            set_out(int(step[1]))
        elif step[0] == "T":
            turn_around([int(d) for d in step[1:]])
        elif step[0] == "S":
            pick_states([int(d) for d in step[1:]])
        else:
            act = {"P": pairs, "R": relay, "Q": second_axis, "U": update, "G": forward, "H": hand_on}
            act[step[0]](int(step[1:]))
    last = [copy for copies in forwards.values() for copy in copies]
    for copy in sent:
        if all(copy is not other for other in last):
            copy.wait_send()
    for copy in last:
        copy.wait_recv()
    for copy in last:
        copy.wait_send()


def fused(grad, first, second, master, old_map, new_map):
    chunks = len(CHUNKS)
    rows = jax.ShapeDtypeStruct((BPD, BLK), f32)
    anywhere = pl.BlockSpec(memory_space=pl.ANY)
    near = pl.BlockSpec(memory_space=pltpu.VMEM)
    sem = pltpu.SemaphoreType.DMA
    return pl.pallas_call(
        kernel,
        out_shape=(rows, rows, rows, jax.ShapeDtypeStruct((8, BPD, BLK), bf16)),
        in_specs=[pl.BlockSpec(memory_space=pltpu.HBM)] * 6,
        out_specs=(near,) * 4,
        scratch_shapes=[
            pltpu.VMEM((3, BPD, BLK), f32),
            pltpu.VMEM((BPD, BPD), jnp.int32),
            pltpu.VMEM((BPD, BPD), jnp.int32),
            pltpu.VMEM((BPD, BPD), jnp.int32),
            pltpu.VMEM((8, BPD, BLK), bf16),
            pltpu.VMEM((8, BPD, BLK), bf16),
            pltpu.VMEM((2, 4, BPD, BLK), bf16),
            pltpu.VMEM((3, 2, BPD, BLK), bf16),
            pltpu.VMEM((4, BPD, BLK), bf16),
            pltpu.VMEM((3, BPD, BLK), bf16),
            pltpu.VMEM((BPD, BLK), f32),
            pltpu.VMEM((2, 2, 8, 8, 3 * BLK // 2), bf16),
            pltpu.VMEM((2, 2, 8, 8, 3 * BLK // 2), bf16),
            pltpu.VMEM((2, 16, 8, 3 * BLK // 2), bf16),
            pltpu.VMEM((2, 16, 8, 3 * BLK // 2), bf16),
            sem((8,)),
            sem((chunks,)), sem((chunks,)),
            sem((chunks, 7)), sem((chunks, 7)),
            sem((2,)), sem((2,)),
            sem((2,)), sem((2,)),
            sem((chunks, 4)), sem((chunks, 4)),
            sem((chunks, 6)), sem((chunks, 6)),
        ],
        compiler_params=pltpu.CompilerParams(
            collective_id=0, has_side_effects=True, vmem_limit_bytes=40000 * 1024
        ),
        name="adamw_relayout",
    )(*[pltpu.with_memory_space_constraint(a, pltpu.HBM) for a in (grad, first, second, master, old_map, new_map)])


def settle(*refs):
    sources, targets, sems = refs[:4], refs[4:8], refs[8]
    copies = [
        pltpu.make_async_copy(sources[3].at[pl.ds(4 * i, 4)], targets[3].at[pl.ds(4 * i, 4)], sems.at[i])
        for i in (0, 1)
    ] + [pltpu.make_async_copy(sources[i], targets[i], sems.at[2 + i]) for i in (0, 1, 2)]
    for copy in copies:
        copy.start()
    for copy in copies:
        copy.wait()


def settled(*arrays):
    anywhere = pl.BlockSpec(memory_space=pl.ANY)
    return pl.pallas_call(
        settle,
        out_shape=tuple(jax.ShapeDtypeStruct(a.shape, a.dtype) for a in arrays),
        in_specs=[anywhere] * 4,
        out_specs=(anywhere,) * 4,
        scratch_shapes=[pltpu.SemaphoreType.DMA((5,))],
        compiler_params=pltpu.CompilerParams(vmem_limit_bytes=1024 * 1024),
        name="settle",
    )(*arrays)


def local(grad_parts, first_moment, second_moment, master, old_map, new_map):
    new_one, new_two, updated, half = settled(*fused(
        grad_parts.reshape(8, 2, BPD, BLK),
        first_moment,
        second_moment,
        master,
        old_map.reshape(BPD, BPD),
        new_map.reshape(BPD, BPD),
    ))
    return (new_one, new_two, updated, half.reshape(8 * BPD, BLK))


def solution(mesh):
    placed = (
        P("dp", None, "shard", None),
        P(("dp", "shard"), None),
        P(("dp", "shard"), None),
        P(("dp", "shard"), None),
        P(),
        P(),
    )
    return jax.shard_map(
        local,
        mesh=mesh,
        in_specs=placed,
        out_specs=(
            P(("dp", "shard"), None),
            P(("dp", "shard"), None),
            P(("dp", "shard"), None),
            P("dp", None),
        ),
        check_vma=False,
    )
```

```python
import functools

import jax
import jax.numpy as jnp
from jax import lax
from jax.experimental import pallas as pl
from jax.experimental.pallas import tpu as pltpu
from jax.sharding import PartitionSpec as P

beta_one = 0.9
beta_two = 0.95
learning_rate = 0.05
decay_rate = 0.1
epsilon = 1e-08
step_count = 4

MESH = pl.DeviceIdType.MESH
BPD = 128
BLK = 1024
f32 = jnp.float32
bf16 = jnp.bfloat16

CHUNKS = ((0, 16, 'x', 'z'), (16, 16, 'x', 'X'), (32, 16, 'x', 'z'), (48, 16, 'y', 'x'), (64, 32, 'Y', 'z'), (96, 32, 'Y', 'X'))
A_MOVES = ((2, 0), (2, 1), (1, 0), (3, 0), (1, 1), (3, 1), (0, 1))
B_MOVES = ((2, 2), (1, 2), (3, 2), (2, 1), (2, 3), (1, 1), (3, 3), (1, 3), (3, 1), (2, 0), (0, 2), (1, 0), (0, 1), (3, 0), (0, 3))
EARLY = (0, 1)
ORDER = (
    "A0", "P1", "A1", "P2", "P4", "P5", "T0", "R4", "R5", "T1", "pick", "Q4",
    "Q5", "P0", "P3", "S0", "S1", "U4", "Q2", "U5", "Q3", "U2", "Q1", "G4",
    "Q0", "G5", "U1", "U3", "U0", "G2", "G1", "G3", "G0", "H5", "H1",
)
PIECES = ((0, 0, 1024, 0, 0), (1, 0, 512, 0, 1024), (1, 512, 512, 1, 0), (2, 0, 1024, 1, 512))


def adamw(moment_one, moment_two, weights, gradient):
    new_one = beta_one * moment_one + (1.0 - beta_one) * gradient
    new_two = beta_two * moment_two + (1.0 - beta_two) * gradient * gradient
    unbiased_one = new_one / (1.0 - beta_one**step_count)
    unbiased_two = new_two / (1.0 - beta_two**step_count)
    updated = weights - learning_rate * (
        unbiased_one / (jnp.sqrt(unbiased_two) + epsilon) + decay_rate * weights
    )
    return (new_one, new_two, updated)


def owners(wanted_row, table_ref, turned_ref):
    wanted = jnp.broadcast_to(wanted_row, (BPD, BPD)).T
    turned_ref[...] = table_ref[...].T

    def step(k, found):
        return jnp.where(wanted == turned_ref[pl.ds(k, 1), :], 1.0, found)

    return lax.fori_loop(0, BPD, step, jnp.zeros((BPD, BPD), f32), unroll=8)


def swap_matrix():
    row = lax.broadcasted_iota(jnp.int32, (BPD, BPD), 0)
    col = lax.broadcasted_iota(jnp.int32, (BPD, BPD), 1)
    turned = (row & 64) | ((row & 7) << 3) | ((row >> 3) & 7)
    return jnp.where(turned == col, 1.0, 0.0).astype(bf16)


def kernel(
    grad, first, second, master, old_map, new_map,
    out_one, out_two, out_master, out_half,
    states, old_ref, new_ref, turned, own, other, pair, from_y, from_x, part, kept,
    send_a, recv_a, send_b, recv_b,
    load_sem, core_s, core_r, sum_s, sum_r, a_s, a_r, b_s, b_r, gat_s, gat_r, fwd_s, fwd_r,
):
    dp = lax.axis_index("dp")
    sh = lax.axis_index("shard")
    xl, yc = dp // 8, dp % 8
    y, c = yc // 2, yc % 2
    xh, z = sh // 4, sh % 4
    me = dp * 8 + sh

    def at_y(k):
        return (xl * 8 + lax.rem(y + k, 4) * 2 + c, sh)

    def at_z(k):
        return (dp, xh * 4 + lax.rem(z + k, 4))

    x_near = ((1 - xl) * 8 + yc, sh)
    x_far = (dp, (1 - xh) * 4 + z)
    core_mate = (xl * 8 + y * 2 + (1 - c), sh)
    a_places = [lax.rem(y + dy, 4) * 2 + lax.rem(c + dc, 2) for dy, dc in A_MOVES]
    a_peers = [(xl * 8 + p, sh) for p in a_places]
    place = xl * 8 + sh
    b_places, b_peers = [], []
    for dx, dz in B_MOVES:
        to_x, to_z = lax.rem(xh * 2 + xl + dx, 4), lax.rem(z + dz, 4)
        b_peers.append((lax.rem(to_x, 2) * 8 + yc, (to_x // 2) * 4 + to_z))
        b_places.append(lax.rem(to_x, 2) * 8 + (to_x // 2) * 4 + to_z)

    barrier = pltpu.get_barrier_semaphore()
    for peer in a_peers + b_peers:
        pl.semaphore_signal(barrier, inc=1, device_id=peer, device_id_type=MESH)

    loads = [
        pltpu.make_async_copy(new_map, new_ref, load_sem.at[0]),
        pltpu.make_async_copy(old_map, old_ref, load_sem.at[1]),
        pltpu.make_async_copy(first, states.at[0], load_sem.at[2]),
        pltpu.make_async_copy(second, states.at[1], load_sem.at[3]),
        pltpu.make_async_copy(master, states.at[2], load_sem.at[4]),
        pltpu.make_async_copy(grad.at[:, c], own, load_sem.at[5]),
    ]
    for load in loads:
        load.start()
    loads[0].wait()
    loads[1].wait()
    swap = swap_matrix()
    route = owners(old_ref[pl.ds(me, 1), :], new_ref, turned).T.astype(bf16)
    routes = (route, jnp.dot(swap, route, preferred_element_type=f32).astype(bf16))

    pending = dict(enumerate(loads[2:6]))

    def set_out(lane):
        for j, c0, w, of, l0 in PIECES:
            if of == lane:
                if j in pending:
                    pending.pop(j).wait()
                moved = jnp.dot(
                    routes[lane], states[j, :, c0 : c0 + w].astype(bf16), preferred_element_type=f32
                )
                if lane == 0:
                    send_a[0, :, :, :, l0 : l0 + w] = moved.reshape(2, 8, 8, w).astype(bf16)
                else:
                    send_b[1, :, :, l0 : l0 + w] = moved.reshape(16, 8, w).astype(bf16)
    for lane in EARLY:
        set_out(lane)
    pl.semaphore_wait(barrier, 22)

    def remote(src, dst, s_sem, r_sem, peer):
        copy = pltpu.make_async_remote_copy(
            src_ref=src, dst_ref=dst, send_sem=s_sem, recv_sem=r_sem,
            device_id=peer, device_id_type=MESH,
        )
        copy.start()
        return copy

    def joined(src, dst, s_sem, r_sem):
        return pltpu.make_async_remote_copy(
            src_ref=src, dst_ref=dst, send_sem=s_sem, recv_sem=r_sem,
            device_id=core_mate, device_id_type=MESH,
        )

    sent = []

    core = {}
    for i in [int(step[1:]) for step in ORDER if step[0] == "P"]:
        rows = pl.ds(*CHUNKS[i][:2])
        core[i] = remote(
            grad.at[:, 1 - c, rows], other.at[:, rows], core_s.at[i], core_r.at[i], core_mate
        )
        sent.append(core[i])


    def over_a(lane):
        for k in range(7):
            (
                remote(
                    send_a.at[lane, :, a_places[k]], recv_a.at[lane, :, yc],
                    a_s.at[lane], a_r.at[lane], a_peers[k],
                )
            )
        whole = pltpu.make_async_remote_copy(
            src_ref=send_a.at[lane, :, pl.ds(0, 7)], dst_ref=recv_a.at[lane, :, pl.ds(0, 7)],
            send_sem=a_s.at[lane], recv_sem=a_r.at[lane], device_id=a_peers[0], device_id_type=MESH,
        )
        keep = pltpu.make_async_copy(send_a.at[lane, :, yc], recv_a.at[lane, :, yc], load_sem.at[lane])
        keep.start()
        return [whole], keep

    def over_b(lane):
        for k in range(15):
            (
                remote(
                    send_b.at[lane, b_places[k]], recv_b.at[lane, place],
                    b_s.at[lane], b_r.at[lane], b_peers[k],
                )
            )
        whole = pltpu.make_async_remote_copy(
            src_ref=send_b.at[lane, pl.ds(0, 15)], dst_ref=recv_b.at[lane, pl.ds(0, 15)],
            send_sem=b_s.at[lane], recv_sem=b_r.at[lane], device_id=b_peers[0], device_id_type=MESH,
        )
        keep = pltpu.make_async_copy(send_b.at[lane, place], recv_b.at[lane, place], load_sem.at[6 + lane])
        keep.start()
        return [whole], keep

    def arrived(stage):
        for copy in stage[0]:
            copy.wait_recv()
        stage[1].wait()

    steps_one, steps_two, gathers, forwards = {}, {}, {}, {}

    def pairs(i):
        r0, n, order, _ = CHUNKS[i]
        rows = pl.ds(r0, n)
        core[i].wait_recv()
        if 3 in pending:
            pending.pop(3).wait()

        def add_pair(q, carry):
            pair[q // 4, q % 4, rows, :] = own[q, rows, :] + other[q, rows, :]
            return carry

        lax.fori_loop(0, 8, add_pair, 0)
        if order == "x":
            copies = [
                remote(pair.at[1 - xl, :, rows], from_x.at[:, rows], sum_s.at[i, 0], sum_r.at[i, 0], x_near)
            ]
        elif order == "d":
            copies = [
                remote(pair.at[1 - xl, y, rows], from_x.at[0, rows], sum_s.at[i, 6], sum_r.at[i, 6], x_near)
            ]
            for k in range(1, 4):
                for side, there in ((0, xl), (1, 1 - xl)):
                    to = lax.rem(y + k, 4)
                    copies.append(
                        remote(
                            pair.at[there, to, rows], from_y.at[k - 1, side, rows],
                            sum_s.at[i, side * 3 + k - 1], sum_r.at[i, side * 3 + k - 1],
                            (there * 8 + to * 2 + c, sh),
                        )
                    )
        elif order == "y":
            for k in (2, 1, 3):
                remote(
                    pair.at[:, lax.rem(y + k, 4), rows], from_y.at[k - 1, :, rows],
                    sum_s.at[i, 0], sum_r.at[i, 0], at_y(k),
                )
            copies = [
                joined(from_y.at[:, :, rows], from_y.at[:, :, rows], sum_s.at[i, 0], sum_r.at[i, 0])
            ]
        else:
            low, high = pl.ds(r0, n // 2), pl.ds(r0 + n // 2, n // 2)
            copies = []
            for k, to, half, slot, peer in (
                (0, 2, low, 1, 1), (1, 2, high, 1, 3), (2, 1, high, 0, 1), (3, 3, low, 2, 3)
            ):
                copies.append(
                    remote(
                        pair.at[:, lax.rem(y + to, 4), half], from_y.at[slot, :, half],
                        sum_s.at[i, k], sum_r.at[i, k], at_y(peer),
                    )
                )
        steps_one[i] = copies
        sent.extend(copies)

    def relay(i):
        r0, n, _, _ = CHUNKS[i]
        for k, to, half in ((0, 1, pl.ds(r0, n // 2)), (1, 3, pl.ds(r0 + n // 2, n // 2))):
            steps_one[i][k].wait_recv()
            place_y = lax.rem(y + to, 4)
            for side in range(2):
                pair[side, place_y, half, :] = pair[side, place_y, half, :] + from_y[1, side, half, :]
            copy = remote(
                pair.at[:, place_y, half], from_y.at[to - 1, :, half],
                sum_s.at[i, 4 + k], sum_r.at[i, 4 + k], at_y(to),
            )
            steps_one[i].append(copy)
            sent.append(copy)
        del steps_one[i][:2]

    def second_axis(i):
        r0, n, order, _ = CHUNKS[i]
        rows = pl.ds(r0, n)
        for copy in steps_one[i]:
            copy.wait_recv()
        copies = []
        if order == "d":
            value = pair[xl, y, rows, :].astype(f32) + from_x[0, rows, :].astype(f32)
            for k in range(3):
                for side in range(2):
                    value = value + from_y[k, side, rows, :].astype(f32)
            kept[rows, :] = value
        elif order == "x":
            for k in (2, 1, 3):
                to = lax.rem(y + k, 4)
                part[k - 1, rows, :] = pair[xl, to, rows, :] + from_x[to, rows, :]
                remote(
                    part.at[k - 1, rows], from_y.at[k - 1, 0, rows],
                    sum_s.at[i, 1], sum_r.at[i, 1], at_y(k),
                )
            copies.append(
                joined(from_y.at[:, 0, rows], from_y.at[:, 0, rows], sum_s.at[i, 1], sum_r.at[i, 1])
            )
            kept[rows, :] = pair[xl, y, rows, :].astype(f32) + from_x[y, rows, :].astype(f32)
        else:
            def total(side):
                value = pair[side, y, rows, :].astype(f32)
                for k in (0, 1, 2) if order == "y" else (0, 2):
                    value = value + from_y[k, side, rows, :].astype(f32)
                return value

            part[0, rows, :] = total(1 - xl).astype(bf16)
            copies.append(
                remote(part.at[0, rows], from_x.at[0, rows], sum_s.at[i, 6], sum_r.at[i, 6], x_near)
            )
            kept[rows, :] = total(xl)
        steps_two[i] = copies
        sent.extend(copies)

    def update(i):
        r0, n, order, gather = CHUNKS[i]
        rows = pl.ds(r0, n)
        for copy in steps_two[i]:
            copy.wait_recv()
        summed = kept[rows, :]
        if order == "d":
            pass
        elif order == "x":
            for k in range(3):
                summed = summed + from_y[k, 0, rows, :].astype(f32)
        else:
            summed = summed + from_x[0, rows, :].astype(f32)
        new_one, new_two, updated = adamw(
            states[0, rows, :], states[1, rows, :], states[2, rows, :], summed
        )
        out_half[sh, rows, :] = updated.astype(bf16)
        block = out_half.at[sh, rows]
        copies = [remote(block, block, gat_s.at[i, 0], gat_r.at[i, 0], x_far)]
        for k in (1, 2, 3) if gather in "xzd" else (1, 3):
            copies.append(remote(block, block, gat_s.at[i, k], gat_r.at[i, k], at_z(k)))
        if gather == "d":
            for k in range(1, 4):
                far = (dp, (1 - xh) * 4 + lax.rem(z + k, 4))
                copies.append(remote(block, block, fwd_s.at[i, k - 1], fwd_r.at[i, k - 1], far))
        gathers[i] = copies
        sent.extend(copies)
        out_one[rows, :] = new_one
        out_two[rows, :] = new_two
        out_master[rows, :] = updated

    def forward(i):
        r0, n, _, order = CHUNKS[i]
        rows, low, high = pl.ds(r0, n), pl.ds(r0, n // 2), pl.ds(r0 + n // 2, n // 2)
        first_copies = gathers[i]
        copies = []

        def send(block, k, peer):
            copies.append(remote(block, block, fwd_s.at[i, k], fwd_r.at[i, k], peer))

        def behind(k):
            return lax.rem(z + 4 - k, 4)

        if order == "d":
            forwards[i] = first_copies
            return
        if order == "x":
            first_copies[0].wait_recv()
            for k in range(1, 4):
                send(out_half.at[(1 - xh) * 4 + z, rows], k - 1, at_z(k))
            for k in range(1, 4):
                first_copies[k].wait_recv()
        elif order == "z":
            for k in range(1, 4):
                first_copies[k].wait_recv()
                send(out_half.at[xh * 4 + behind(k), rows], k - 1, x_far)
            first_copies[0].wait_recv()
        elif order == "X":
            first_copies[0].wait_recv()
            for k, peer in ((0, 1), (1, 3)):
                send(out_half.at[(1 - xh) * 4 + z, rows], k, at_z(peer))
            for k, peer, half in ((1, 1, low), (2, 3, high)):
                first_copies[k].wait_recv()
                send(out_half.at[xh * 4 + behind(peer), half], k + 1, at_z(peer))
        else:
            for k, peer, half in ((1, 1, low), (2, 3, high)):
                first_copies[k].wait_recv()
                send(out_half.at[xh * 4 + behind(peer), half], k - 1, at_z(peer))
                send(out_half.at[xh * 4 + behind(peer), rows], k + 1, x_far)
            first_copies[0].wait_recv()
        forwards[i] = copies
        sent.extend(copies)

    def hand_on(i):
        r0, n, _, order = CHUNKS[i]
        rows, low, high = pl.ds(r0, n), pl.ds(r0, n // 2), pl.ds(r0 + n // 2, n // 2)
        copies = []
        if order == "X":
            for k, peer, half in ((0, 1, low), (1, 3, high)):
                forwards[i][k].wait_recv()
                block = out_half.at[(1 - xh) * 4 + lax.rem(z + 4 - peer, 4), half]
                copies.append(remote(block, block, fwd_s.at[i, 4 + k], fwd_r.at[i, 4 + k], at_z(peer)))
        else:
            for k in range(2):
                forwards[i][k].wait_recv()
            block = out_half.at[xh * 4 + lax.rem(z + 2, 4), rows]
            copies.append(remote(block, block, fwd_s.at[i, 4], fwd_r.at[i, 4], x_far))
        forwards[i] = forwards[i][2:] + copies
        sent.extend(copies)

    def turn_around(lanes):
        for lane in lanes:
            arrived(stage_one[lane])
            for _, _, w, of, l0 in PIECES:
                if of == lane:
                    source = recv_a[0, :, :, :, l0 : l0 + w] if lane == 0 else recv_b[1, :, :, l0 : l0 + w]
                    came = source.astype(f32).reshape(BPD, w).astype(bf16)
                    moved = jnp.dot(swap, came, preferred_element_type=f32)
                    if lane == 0:
                        send_b[0, :, :, l0 : l0 + w] = moved.reshape(16, 8, w).astype(bf16)
                    else:
                        send_a[1, :, :, :, l0 : l0 + w] = moved.reshape(2, 8, 8, w).astype(bf16)
            stage_two[lane] = over_b(0) if lane == 0 else over_a(1)
            sent.extend(stage_two[lane][0])

    def pick_states(lanes):
        for lane in lanes:
            arrived(stage_two[lane])
            for j, c0, w, of, l0 in PIECES:
                if of == lane:
                    source = recv_b[0, :, :, l0 : l0 + w] if lane == 0 else recv_a[1, :, :, :, l0 : l0 + w]
                    came = source.astype(f32).reshape(BPD, w).astype(bf16)
                    states[j, :, c0 : c0 + w] = jnp.dot(picks[lane], came, preferred_element_type=f32)

    stage_one, stage_two, picks = {}, {}, []
    for step in ORDER:
        if step == "pick":
            pick = owners(new_ref[pl.ds(me, 1), :], old_ref, turned).astype(bf16)
            picks += [jnp.dot(pick, swap, preferred_element_type=f32).astype(bf16), pick]
        elif step[0] == "A":
            lane = int(step[1])
            if lane not in EARLY:
                set_out(lane)
            stage_one[lane] = over_a(0) if lane == 0 else over_b(1)
            sent.extend(stage_one[lane][0])
        elif step[0] == "T":
            turn_around([int(d) for d in step[1:]])
        elif step[0] == "S":
            pick_states([int(d) for d in step[1:]])
        else:
            act = {"P": pairs, "R": relay, "Q": second_axis, "U": update, "G": forward, "H": hand_on}
            act[step[0]](int(step[1:]))
    last = [copy for copies in forwards.values() for copy in copies]
    for copy in sent:
        if all(copy is not other for other in last):
            copy.wait_send()
    for copy in last:
        copy.wait_recv()
    for copy in last:
        copy.wait_send()


def fused(grad, first, second, master, old_map, new_map):
    chunks = len(CHUNKS)
    rows = jax.ShapeDtypeStruct((BPD, BLK), f32)
    anywhere = pl.BlockSpec(memory_space=pl.ANY)
    near = pl.BlockSpec(memory_space=pltpu.VMEM)
    sem = pltpu.SemaphoreType.DMA
    return pl.pallas_call(
        kernel,
        out_shape=(rows, rows, rows, jax.ShapeDtypeStruct((8, BPD, BLK), bf16)),
        in_specs=[pl.BlockSpec(memory_space=pltpu.HBM)] * 6,
        out_specs=(near,) * 4,
        scratch_shapes=[
            pltpu.VMEM((3, BPD, BLK), f32),
            pltpu.VMEM((BPD, BPD), jnp.int32),
            pltpu.VMEM((BPD, BPD), jnp.int32),
            pltpu.VMEM((BPD, BPD), jnp.int32),
            pltpu.VMEM((8, BPD, BLK), bf16),
            pltpu.VMEM((8, BPD, BLK), bf16),
            pltpu.VMEM((2, 4, BPD, BLK), bf16),
            pltpu.VMEM((3, 2, BPD, BLK), bf16),
            pltpu.VMEM((4, BPD, BLK), bf16),
            pltpu.VMEM((3, BPD, BLK), bf16),
            pltpu.VMEM((BPD, BLK), f32),
            pltpu.VMEM((2, 2, 8, 8, 3 * BLK // 2), bf16),
            pltpu.VMEM((2, 2, 8, 8, 3 * BLK // 2), bf16),
            pltpu.VMEM((2, 16, 8, 3 * BLK // 2), bf16),
            pltpu.VMEM((2, 16, 8, 3 * BLK // 2), bf16),
            sem((8,)),
            sem((chunks,)), sem((chunks,)),
            sem((chunks, 7)), sem((chunks, 7)),
            sem((2,)), sem((2,)),
            sem((2,)), sem((2,)),
            sem((chunks, 4)), sem((chunks, 4)),
            sem((chunks, 6)), sem((chunks, 6)),
        ],
        compiler_params=pltpu.CompilerParams(
            collective_id=0, has_side_effects=True, vmem_limit_bytes=40000 * 1024
        ),
        name="adamw_relayout",
    )(*[pltpu.with_memory_space_constraint(a, pltpu.HBM) for a in (grad, first, second, master, old_map, new_map)])


def settle(*refs):
    sources, targets, sems = refs[:4], refs[4:8], refs[8]
    copies = [
        pltpu.make_async_copy(sources[3].at[pl.ds(4 * i, 4)], targets[3].at[pl.ds(4 * i, 4)], sems.at[i])
        for i in (0, 1)
    ] + [pltpu.make_async_copy(sources[i], targets[i], sems.at[2 + i]) for i in (0, 1, 2)]
    for copy in copies:
        copy.start()
    for copy in copies:
        copy.wait()


def settled(*arrays):
    anywhere = pl.BlockSpec(memory_space=pl.ANY)
    return pl.pallas_call(
        settle,
        out_shape=tuple(jax.ShapeDtypeStruct(a.shape, a.dtype) for a in arrays),
        in_specs=[anywhere] * 4,
        out_specs=(anywhere,) * 4,
        scratch_shapes=[pltpu.SemaphoreType.DMA((5,))],
        compiler_params=pltpu.CompilerParams(vmem_limit_bytes=1024 * 1024),
        name="settle",
    )(*arrays)


def local(grad_parts, first_moment, second_moment, master, old_map, new_map):
    new_one, new_two, updated, half = settled(*fused(
        grad_parts.reshape(8, 2, BPD, BLK),
        first_moment,
        second_moment,
        master,
        old_map.reshape(BPD, BPD),
        new_map.reshape(BPD, BPD),
    ))
    return (new_one, new_two, updated, half.reshape(8 * BPD, BLK))


def solution(mesh):
    placed = (
        P("dp", None, "shard", None),
        P(("dp", "shard"), None),
        P(("dp", "shard"), None),
        P(("dp", "shard"), None),
        P(),
        P(),
    )
    return jax.shard_map(
        local,
        mesh=mesh,
        in_specs=placed,
        out_specs=(
            P(("dp", "shard"), None),
            P(("dp", "shard"), None),
            P(("dp", "shard"), None),
            P("dp", None),
        ),
        check_vma=False,
    )
```

```python
import functools

import jax
import jax.numpy as jnp
from jax import lax
from jax.experimental import pallas as pl
from jax.experimental.pallas import tpu as pltpu
from jax.sharding import PartitionSpec as P

beta_one = 0.9
beta_two = 0.95
learning_rate = 0.05
decay_rate = 0.1
epsilon = 1e-08
step_count = 4

MESH = pl.DeviceIdType.MESH
BPD = 128
BLK = 1024
f32 = jnp.float32
bf16 = jnp.bfloat16

CHUNKS = ((0, 16, 'x', 'z'), (16, 16, 'x', 'X'), (32, 16, 'x', 'z'), (48, 16, 'y', 'x'), (64, 32, 'Y', 'z'), (96, 32, 'Y', 'X'))
A_MOVES = ((2, 0), (2, 1), (1, 0), (3, 0), (1, 1), (3, 1), (0, 1))
B_MOVES = ((2, 2), (1, 2), (3, 2), (2, 1), (2, 3), (1, 1), (3, 3), (1, 3), (3, 1), (2, 0), (0, 2), (1, 0), (0, 1), (3, 0), (0, 3))
EARLY = (0, 1)
ORDER = (
    "A0", "P1", "A1", "P2", "P4", "P5", "T0", "R4", "R5", "T1", "pick", "Q4",
    "Q5", "P0", "P3", "S0", "S1", "U4", "Q2", "U5", "Q3", "U2", "Q1", "G4",
    "Q0", "G5", "U1", "U3", "U0", "G2", "G1", "G3", "G0", "H5", "H1",
)
PIECES = ((0, 0, 1024, 0, 0), (1, 0, 512, 0, 1024), (1, 512, 512, 1, 0), (2, 0, 1024, 1, 512))


def adamw(moment_one, moment_two, weights, gradient):
    new_one = beta_one * moment_one + (1.0 - beta_one) * gradient
    new_two = beta_two * moment_two + (1.0 - beta_two) * gradient * gradient
    unbiased_one = new_one / (1.0 - beta_one**step_count)
    unbiased_two = new_two / (1.0 - beta_two**step_count)
    updated = weights - learning_rate * (
        unbiased_one / (jnp.sqrt(unbiased_two) + epsilon) + decay_rate * weights
    )
    return (new_one, new_two, updated)


def owners(wanted_row, table_ref, turned_ref):
    wanted = jnp.broadcast_to(wanted_row, (BPD, BPD)).T
    turned_ref[...] = table_ref[...].T

    def step(k, found):
        return jnp.where(wanted == turned_ref[pl.ds(k, 1), :], 1.0, found)

    return lax.fori_loop(0, BPD, step, jnp.zeros((BPD, BPD), f32), unroll=8)


def swap_matrix():
    row = lax.broadcasted_iota(jnp.int32, (BPD, BPD), 0)
    col = lax.broadcasted_iota(jnp.int32, (BPD, BPD), 1)
    turned = (row & 64) | ((row & 7) << 3) | ((row >> 3) & 7)
    return jnp.where(turned == col, 1.0, 0.0).astype(bf16)


def kernel(
    grad, first, second, master, old_map, new_map,
    out_one, out_two, out_master, out_half,
    states, old_ref, new_ref, turned, own, other, pair, from_y, from_x, part, kept,
    send_a, recv_a, send_b, recv_b,
    load_sem, core_s, core_r, sum_s, sum_r, a_s, a_r, b_s, b_r, gat_s, gat_r, fwd_s, fwd_r,
):
    dp = lax.axis_index("dp")
    sh = lax.axis_index("shard")
    xl, yc = dp // 8, dp % 8
    y, c = yc // 2, yc % 2
    xh, z = sh // 4, sh % 4
    me = dp * 8 + sh

    def at_y(k):
        return (xl * 8 + lax.rem(y + k, 4) * 2 + c, sh)

    def at_z(k):
        return (dp, xh * 4 + lax.rem(z + k, 4))

    x_near = ((1 - xl) * 8 + yc, sh)
    x_far = (dp, (1 - xh) * 4 + z)
    core_mate = (xl * 8 + y * 2 + (1 - c), sh)
    a_places = [lax.rem(y + dy, 4) * 2 + lax.rem(c + dc, 2) for dy, dc in A_MOVES]
    a_peers = [(xl * 8 + p, sh) for p in a_places]
    place = xl * 8 + sh
    b_places, b_peers = [], []
    for dx, dz in B_MOVES:
        to_x, to_z = lax.rem(xh * 2 + xl + dx, 4), lax.rem(z + dz, 4)
        b_peers.append((lax.rem(to_x, 2) * 8 + yc, (to_x // 2) * 4 + to_z))
        b_places.append(lax.rem(to_x, 2) * 8 + (to_x // 2) * 4 + to_z)

    barrier = pltpu.get_barrier_semaphore()
    for peer in a_peers + b_peers:
        pl.semaphore_signal(barrier, inc=1, device_id=peer, device_id_type=MESH)

    loads = [
        pltpu.make_async_copy(new_map, new_ref, load_sem.at[0]),
        pltpu.make_async_copy(old_map, old_ref, load_sem.at[1]),
        pltpu.make_async_copy(first, states.at[0], load_sem.at[2]),
        pltpu.make_async_copy(second, states.at[1], load_sem.at[3]),
        pltpu.make_async_copy(master, states.at[2], load_sem.at[4]),
        pltpu.make_async_copy(grad.at[:, c], own, load_sem.at[5]),
    ]
    for load in loads:
        load.start()
    loads[0].wait()
    loads[1].wait()
    swap = swap_matrix()
    route = owners(old_ref[pl.ds(me, 1), :], new_ref, turned).T.astype(bf16)
    routes = (route, jnp.dot(swap, route, preferred_element_type=f32).astype(bf16))

    pending = dict(enumerate(loads[2:6]))

    def set_out(lane):
        for j, c0, w, of, l0 in PIECES:
            if of == lane:
                if j in pending:
                    pending.pop(j).wait()
                moved = jnp.dot(
                    routes[lane], states[j, :, c0 : c0 + w].astype(bf16), preferred_element_type=f32
                )
                if lane == 0:
                    send_a[0, :, :, :, l0 : l0 + w] = moved.reshape(2, 8, 8, w).astype(bf16)
                else:
                    send_b[1, :, :, l0 : l0 + w] = moved.reshape(16, 8, w).astype(bf16)
    for lane in EARLY:
        set_out(lane)
    pl.semaphore_wait(barrier, 22)

    def remote(src, dst, s_sem, r_sem, peer):
        copy = pltpu.make_async_remote_copy(
            src_ref=src, dst_ref=dst, send_sem=s_sem, recv_sem=r_sem,
            device_id=peer, device_id_type=MESH,
        )
        copy.start()
        return copy

    def joined(src, dst, s_sem, r_sem):
        return pltpu.make_async_remote_copy(
            src_ref=src, dst_ref=dst, send_sem=s_sem, recv_sem=r_sem,
            device_id=core_mate, device_id_type=MESH,
        )

    sent = []

    def over_a(lane):
        for k in range(7):
            (
                remote(
                    send_a.at[lane, :, a_places[k]], recv_a.at[lane, :, yc],
                    a_s.at[lane], a_r.at[lane], a_peers[k],
                )
            )
        whole = pltpu.make_async_remote_copy(
            src_ref=send_a.at[lane, :, pl.ds(0, 7)], dst_ref=recv_a.at[lane, :, pl.ds(0, 7)],
            send_sem=a_s.at[lane], recv_sem=a_r.at[lane], device_id=a_peers[0], device_id_type=MESH,
        )
        keep = pltpu.make_async_copy(send_a.at[lane, :, yc], recv_a.at[lane, :, yc], load_sem.at[lane])
        keep.start()
        return [whole], keep

    def over_b(lane):
        for k in range(15):
            (
                remote(
                    send_b.at[lane, b_places[k]], recv_b.at[lane, place],
                    b_s.at[lane], b_r.at[lane], b_peers[k],
                )
            )
        whole = pltpu.make_async_remote_copy(
            src_ref=send_b.at[lane, pl.ds(0, 15)], dst_ref=recv_b.at[lane, pl.ds(0, 15)],
            send_sem=b_s.at[lane], recv_sem=b_r.at[lane], device_id=b_peers[0], device_id_type=MESH,
        )
        keep = pltpu.make_async_copy(send_b.at[lane, place], recv_b.at[lane, place], load_sem.at[6 + lane])
        keep.start()
        return [whole], keep

    def arrived(stage):
        for copy in stage[0]:
            copy.wait_recv()
        stage[1].wait()

    stage_one = {}
    for lane in (0, 1):
        stage_one[lane] = over_a(0) if lane == 0 else over_b(1)
        sent.extend(stage_one[lane][0])

    core = {}
    for i in [int(step[1:]) for step in ORDER if step[0] == "P"]:
        rows = pl.ds(*CHUNKS[i][:2])
        core[i] = remote(
            grad.at[:, 1 - c, rows], other.at[:, rows], core_s.at[i], core_r.at[i], core_mate
        )
        sent.append(core[i])


    steps_one, steps_two, gathers, forwards = {}, {}, {}, {}

    def pairs(i):
        r0, n, order, _ = CHUNKS[i]
        rows = pl.ds(r0, n)
        core[i].wait_recv()
        if 3 in pending:
            pending.pop(3).wait()

        def add_pair(q, carry):
            pair[q // 4, q % 4, rows, :] = own[q, rows, :] + other[q, rows, :]
            return carry

        lax.fori_loop(0, 8, add_pair, 0)
        if order == "x":
            copies = [
                remote(pair.at[1 - xl, :, rows], from_x.at[:, rows], sum_s.at[i, 0], sum_r.at[i, 0], x_near)
            ]
        elif order == "d":
            copies = [
                remote(pair.at[1 - xl, y, rows], from_x.at[0, rows], sum_s.at[i, 6], sum_r.at[i, 6], x_near)
            ]
            for k in range(1, 4):
                for side, there in ((0, xl), (1, 1 - xl)):
                    to = lax.rem(y + k, 4)
                    copies.append(
                        remote(
                            pair.at[there, to, rows], from_y.at[k - 1, side, rows],
                            sum_s.at[i, side * 3 + k - 1], sum_r.at[i, side * 3 + k - 1],
                            (there * 8 + to * 2 + c, sh),
                        )
                    )
        elif order == "y":
            for k in (2, 1, 3):
                remote(
                    pair.at[:, lax.rem(y + k, 4), rows], from_y.at[k - 1, :, rows],
                    sum_s.at[i, 0], sum_r.at[i, 0], at_y(k),
                )
            copies = [
                joined(from_y.at[:, :, rows], from_y.at[:, :, rows], sum_s.at[i, 0], sum_r.at[i, 0])
            ]
        else:
            low, high = pl.ds(r0, n // 2), pl.ds(r0 + n // 2, n // 2)
            copies = []
            for k, to, half, slot, peer in (
                (0, 2, low, 1, 1), (1, 2, high, 1, 3), (2, 1, high, 0, 1), (3, 3, low, 2, 3)
            ):
                copies.append(
                    remote(
                        pair.at[:, lax.rem(y + to, 4), half], from_y.at[slot, :, half],
                        sum_s.at[i, k], sum_r.at[i, k], at_y(peer),
                    )
                )
        steps_one[i] = copies
        sent.extend(copies)

    def relay(i):
        r0, n, _, _ = CHUNKS[i]
        for k, to, half in ((0, 1, pl.ds(r0, n // 2)), (1, 3, pl.ds(r0 + n // 2, n // 2))):
            steps_one[i][k].wait_recv()
            place_y = lax.rem(y + to, 4)
            for side in range(2):
                pair[side, place_y, half, :] = pair[side, place_y, half, :] + from_y[1, side, half, :]
            copy = remote(
                pair.at[:, place_y, half], from_y.at[to - 1, :, half],
                sum_s.at[i, 4 + k], sum_r.at[i, 4 + k], at_y(to),
            )
            steps_one[i].append(copy)
            sent.append(copy)
        del steps_one[i][:2]

    def second_axis(i):
        r0, n, order, _ = CHUNKS[i]
        rows = pl.ds(r0, n)
        for copy in steps_one[i]:
            copy.wait_recv()
        copies = []
        if order == "d":
            value = pair[xl, y, rows, :].astype(f32) + from_x[0, rows, :].astype(f32)
            for k in range(3):
                for side in range(2):
                    value = value + from_y[k, side, rows, :].astype(f32)
            kept[rows, :] = value
        elif order == "x":
            for k in (2, 1, 3):
                to = lax.rem(y + k, 4)
                part[k - 1, rows, :] = pair[xl, to, rows, :] + from_x[to, rows, :]
                remote(
                    part.at[k - 1, rows], from_y.at[k - 1, 0, rows],
                    sum_s.at[i, 1], sum_r.at[i, 1], at_y(k),
                )
            copies.append(
                joined(from_y.at[:, 0, rows], from_y.at[:, 0, rows], sum_s.at[i, 1], sum_r.at[i, 1])
            )
            kept[rows, :] = pair[xl, y, rows, :].astype(f32) + from_x[y, rows, :].astype(f32)
        else:
            def total(side):
                value = pair[side, y, rows, :].astype(f32)
                for k in (0, 1, 2) if order == "y" else (0, 2):
                    value = value + from_y[k, side, rows, :].astype(f32)
                return value

            part[0, rows, :] = total(1 - xl).astype(bf16)
            copies.append(
                remote(part.at[0, rows], from_x.at[0, rows], sum_s.at[i, 6], sum_r.at[i, 6], x_near)
            )
            kept[rows, :] = total(xl)
        steps_two[i] = copies
        sent.extend(copies)

    def update(i):
        r0, n, order, gather = CHUNKS[i]
        rows = pl.ds(r0, n)
        for copy in steps_two[i]:
            copy.wait_recv()
        summed = kept[rows, :]
        if order == "d":
            pass
        elif order == "x":
            for k in range(3):
                summed = summed + from_y[k, 0, rows, :].astype(f32)
        else:
            summed = summed + from_x[0, rows, :].astype(f32)
        new_one, new_two, updated = adamw(
            states[0, rows, :], states[1, rows, :], states[2, rows, :], summed
        )
        out_half[sh, rows, :] = updated.astype(bf16)
        block = out_half.at[sh, rows]
        copies = [remote(block, block, gat_s.at[i, 0], gat_r.at[i, 0], x_far)]
        for k in (1, 2, 3) if gather in "xzd" else (1, 3):
            copies.append(remote(block, block, gat_s.at[i, k], gat_r.at[i, k], at_z(k)))
        if gather == "d":
            for k in range(1, 4):
                far = (dp, (1 - xh) * 4 + lax.rem(z + k, 4))
                copies.append(remote(block, block, fwd_s.at[i, k - 1], fwd_r.at[i, k - 1], far))
        gathers[i] = copies
        sent.extend(copies)
        out_one[rows, :] = new_one
        out_two[rows, :] = new_two
        out_master[rows, :] = updated

    def forward(i):
        r0, n, _, order = CHUNKS[i]
        rows, low, high = pl.ds(r0, n), pl.ds(r0, n // 2), pl.ds(r0 + n // 2, n // 2)
        first_copies = gathers[i]
        copies = []

        def send(block, k, peer):
            copies.append(remote(block, block, fwd_s.at[i, k], fwd_r.at[i, k], peer))

        def behind(k):
            return lax.rem(z + 4 - k, 4)

        if order == "d":
            forwards[i] = first_copies
            return
        if order == "x":
            first_copies[0].wait_recv()
            for k in range(1, 4):
                send(out_half.at[(1 - xh) * 4 + z, rows], k - 1, at_z(k))
            for k in range(1, 4):
                first_copies[k].wait_recv()
        elif order == "z":
            for k in range(1, 4):
                first_copies[k].wait_recv()
                send(out_half.at[xh * 4 + behind(k), rows], k - 1, x_far)
            first_copies[0].wait_recv()
        elif order == "X":
            first_copies[0].wait_recv()
            for k, peer in ((0, 1), (1, 3)):
                send(out_half.at[(1 - xh) * 4 + z, rows], k, at_z(peer))
            for k, peer, half in ((1, 1, low), (2, 3, high)):
                first_copies[k].wait_recv()
                send(out_half.at[xh * 4 + behind(peer), half], k + 1, at_z(peer))
        else:
            for k, peer, half in ((1, 1, low), (2, 3, high)):
                first_copies[k].wait_recv()
                send(out_half.at[xh * 4 + behind(peer), half], k - 1, at_z(peer))
                send(out_half.at[xh * 4 + behind(peer), rows], k + 1, x_far)
            first_copies[0].wait_recv()
        forwards[i] = copies
        sent.extend(copies)

    def hand_on(i):
        r0, n, _, order = CHUNKS[i]
        rows, low, high = pl.ds(r0, n), pl.ds(r0, n // 2), pl.ds(r0 + n // 2, n // 2)
        copies = []
        if order == "X":
            for k, peer, half in ((0, 1, low), (1, 3, high)):
                forwards[i][k].wait_recv()
                block = out_half.at[(1 - xh) * 4 + lax.rem(z + 4 - peer, 4), half]
                copies.append(remote(block, block, fwd_s.at[i, 4 + k], fwd_r.at[i, 4 + k], at_z(peer)))
        else:
            for k in range(2):
                forwards[i][k].wait_recv()
            block = out_half.at[xh * 4 + lax.rem(z + 2, 4), rows]
            copies.append(remote(block, block, fwd_s.at[i, 4], fwd_r.at[i, 4], x_far))
        forwards[i] = forwards[i][2:] + copies
        sent.extend(copies)

    def turn_around(lanes):
        for lane in lanes:
            arrived(stage_one[lane])
            for _, _, w, of, l0 in PIECES:
                if of == lane:
                    source = recv_a[0, :, :, :, l0 : l0 + w] if lane == 0 else recv_b[1, :, :, l0 : l0 + w]
                    came = source.astype(f32).reshape(BPD, w).astype(bf16)
                    moved = jnp.dot(swap, came, preferred_element_type=f32)
                    if lane == 0:
                        send_b[0, :, :, l0 : l0 + w] = moved.reshape(16, 8, w).astype(bf16)
                    else:
                        send_a[1, :, :, :, l0 : l0 + w] = moved.reshape(2, 8, 8, w).astype(bf16)
            stage_two[lane] = over_b(0) if lane == 0 else over_a(1)
            sent.extend(stage_two[lane][0])

    def pick_states(lanes):
        for lane in lanes:
            arrived(stage_two[lane])
            for j, c0, w, of, l0 in PIECES:
                if of == lane:
                    source = recv_b[0, :, :, l0 : l0 + w] if lane == 0 else recv_a[1, :, :, :, l0 : l0 + w]
                    came = source.astype(f32).reshape(BPD, w).astype(bf16)
                    states[j, :, c0 : c0 + w] = jnp.dot(picks[lane], came, preferred_element_type=f32)

    stage_two, picks = {}, []
    for step in ORDER:
        if step == "pick":
            pick = owners(new_ref[pl.ds(me, 1), :], old_ref, turned).astype(bf16)
            picks += [jnp.dot(pick, swap, preferred_element_type=f32).astype(bf16), pick]
        elif step[0] == "A":
            lane = int(step[1])
            if lane not in EARLY:
                set_out(lane)
            if lane not in stage_one:
                stage_one[lane] = over_a(0) if lane == 0 else over_b(1)
                sent.extend(stage_one[lane][0])
        elif step[0] == "T":
            turn_around([int(d) for d in step[1:]])
        elif step[0] == "S":
            pick_states([int(d) for d in step[1:]])
        else:
            act = {"P": pairs, "R": relay, "Q": second_axis, "U": update, "G": forward, "H": hand_on}
            act[step[0]](int(step[1:]))
    last = [copy for copies in forwards.values() for copy in copies]
    for copy in sent:
        if all(copy is not other for other in last):
            copy.wait_send()
    for copy in last:
        copy.wait_recv()
    for copy in last:
        copy.wait_send()


def fused(grad, first, second, master, old_map, new_map):
    chunks = len(CHUNKS)
    rows = jax.ShapeDtypeStruct((BPD, BLK), f32)
    anywhere = pl.BlockSpec(memory_space=pl.ANY)
    near = pl.BlockSpec(memory_space=pltpu.VMEM)
    sem = pltpu.SemaphoreType.DMA
    return pl.pallas_call(
        kernel,
        out_shape=(rows, rows, rows, jax.ShapeDtypeStruct((8, BPD, BLK), bf16)),
        in_specs=[pl.BlockSpec(memory_space=pltpu.HBM)] * 6,
        out_specs=(near,) * 4,
        scratch_shapes=[
            pltpu.VMEM((3, BPD, BLK), f32),
            pltpu.VMEM((BPD, BPD), jnp.int32),
            pltpu.VMEM((BPD, BPD), jnp.int32),
            pltpu.VMEM((BPD, BPD), jnp.int32),
            pltpu.VMEM((8, BPD, BLK), bf16),
            pltpu.VMEM((8, BPD, BLK), bf16),
            pltpu.VMEM((2, 4, BPD, BLK), bf16),
            pltpu.VMEM((3, 2, BPD, BLK), bf16),
            pltpu.VMEM((4, BPD, BLK), bf16),
            pltpu.VMEM((3, BPD, BLK), bf16),
            pltpu.VMEM((BPD, BLK), f32),
            pltpu.VMEM((2, 2, 8, 8, 3 * BLK // 2), bf16),
            pltpu.VMEM((2, 2, 8, 8, 3 * BLK // 2), bf16),
            pltpu.VMEM((2, 16, 8, 3 * BLK // 2), bf16),
            pltpu.VMEM((2, 16, 8, 3 * BLK // 2), bf16),
            sem((8,)),
            sem((chunks,)), sem((chunks,)),
            sem((chunks, 7)), sem((chunks, 7)),
            sem((2,)), sem((2,)),
            sem((2,)), sem((2,)),
            sem((chunks, 4)), sem((chunks, 4)),
            sem((chunks, 6)), sem((chunks, 6)),
        ],
        compiler_params=pltpu.CompilerParams(
            collective_id=0, has_side_effects=True, vmem_limit_bytes=40000 * 1024
        ),
        name="adamw_relayout",
    )(*[pltpu.with_memory_space_constraint(a, pltpu.HBM) for a in (grad, first, second, master, old_map, new_map)])


def settle(*refs):
    sources, targets, sems = refs[:4], refs[4:8], refs[8]
    copies = [
        pltpu.make_async_copy(sources[3].at[pl.ds(4 * i, 4)], targets[3].at[pl.ds(4 * i, 4)], sems.at[i])
        for i in (0, 1)
    ] + [pltpu.make_async_copy(sources[i], targets[i], sems.at[2 + i]) for i in (0, 1, 2)]
    for copy in copies:
        copy.start()
    for copy in copies:
        copy.wait()


def settled(*arrays):
    anywhere = pl.BlockSpec(memory_space=pl.ANY)
    return pl.pallas_call(
        settle,
        out_shape=tuple(jax.ShapeDtypeStruct(a.shape, a.dtype) for a in arrays),
        in_specs=[anywhere] * 4,
        out_specs=(anywhere,) * 4,
        scratch_shapes=[pltpu.SemaphoreType.DMA((5,))],
        compiler_params=pltpu.CompilerParams(vmem_limit_bytes=1024 * 1024),
        name="settle",
    )(*arrays)


def local(grad_parts, first_moment, second_moment, master, old_map, new_map):
    new_one, new_two, updated, half = settled(*fused(
        grad_parts.reshape(8, 2, BPD, BLK),
        first_moment,
        second_moment,
        master,
        old_map.reshape(BPD, BPD),
        new_map.reshape(BPD, BPD),
    ))
    return (new_one, new_two, updated, half.reshape(8 * BPD, BLK))


def solution(mesh):
    placed = (
        P("dp", None, "shard", None),
        P(("dp", "shard"), None),
        P(("dp", "shard"), None),
        P(("dp", "shard"), None),
        P(),
        P(),
    )
    return jax.shard_map(
        local,
        mesh=mesh,
        in_specs=placed,
        out_specs=(
            P(("dp", "shard"), None),
            P(("dp", "shard"), None),
            P(("dp", "shard"), None),
            P("dp", None),
        ),
        check_vma=False,
    )
```
